768 devices in a mesh: edp: 48 (over z, x_lo, core), ep: 16 (over y, x_hi).
Axes of the slice: x: 4 (x_hi: 2, x_lo: 2; x = x_hi * 2 + x_lo), y: 8, z: 12, core: 2. Of those that a mesh axis runs over, the one named last changes fastest.
Arguments:
- route_ids: int32 [98304, 8], P(('edp', 'ep')), may hold values from 0 to 127, all different within a row; in each aligned block of 128 rows (0 to 127, 128 to 255, ...) at most 16 rows name the same one
- route_weights: float32 [98304, 8], P(('edp', 'ep')), may hold values from 0.02 to 0.5
- hidden: bfloat16 [48, 16, 16, 16, 384], P('edp', 'ep'), may hold values from -6 to 6
- down_weight: bfloat16 [16, 384, 2048], P('ep', 'edp'), may hold values from -0.3125 to 0.3125
- cotangent: bfloat16 [98304, 2048], P(('edp', 'ep')), may hold values from -6 to 6
Outputs:
- layer_out: bfloat16 [98304, 2048], P(('edp', 'ep'))
- route_grad: float32 [98304, 8], P(('edp', 'ep'))
- hidden_grad: bfloat16 [48, 16, 16, 16, 384], P('edp', 'ep')
- weight_grad: float32 [16, 384, 2048], P('ep', 'edp')
The draws below stay inside these ranges and needn't reach their ends.
Inputs may be any that keep to these rules, and one draw needn't show every extreme that they name: `route_ids`: each row names 8 different experts; in the 128 rows of one device no expert is named by more than 16 rows.
All inputs are finite; a program needn't handle non-finite values.
Results may differ from the reference program's by a relative error of at most 0.0049.
Values may be sent and summed in bfloat16 or wider, within the bound.
A program may use at most 32 MiB of HBM per device.

```python
import math
import jax
import jax.numpy as jnp
import numpy as np
from jax import lax

D = 2048
EXPERTS = 128
TOP = 8
FF = 384
TOK_DEV = 128
CAP = 16
WIN = 16
TOKENS = 98304
N_EDP = 48
N_EP = 16


def spiked(values, stream_key, source, target, shards_of, factor):
    owner, partner = [(jnp.arange(values.shape[position]) // (values.shape[position] // shards_of)).reshape([-1 if axis == position else 1 for axis in range(values.ndim)]) for position in (source, target)]
    chosen = jax.random.permutation(stream_key, shards_of)[partner]
    strong = (owner == chosen) | (owner == (partner + shards_of // 2) % shards_of)
    return jnp.where(strong, factor * values, values)


def levels(key, shape, split, smallest, largest):
    def one(dim, blocks):
        steps = jax.random.uniform(jax.random.fold_in(jax.random.fold_in(key, 6), dim), (blocks,), jnp.float32, smallest / len(split), largest / len(split))
        return jnp.repeat(jnp.exp(steps), shape[dim] // blocks).reshape((-1,) + (1,) * (len(shape) - dim - 1))

    factor_of = one(*split[0])
    for cut in split[1:]:
        factor_of = factor_of * one(*cut)
    return factor_of


def shared_out(key, own, number, rows, amount, top, bound, lean):
    order = jax.random.permutation(key, amount)
    packed, common = shares(amount, rows * top, bound, lean, True), shares(amount, rows * top, bound, lean, False)
    places = jnp.arange(amount)

    def named(sizes, rotation):
        used = int((sizes > 0).sum())
        fixed = max(1, used // 4)
        passed = fixed + (places - fixed + rotation * (used - fixed)) % max(1, amount - fixed)
        return jnp.zeros((amount,), jnp.int32).at[order[jnp.where(places < fixed, places, passed)]].set(jnp.asarray(sizes, jnp.int32))

    sizes = jnp.where(number % 4 == 0, named(packed, number // 4), named(common, number - number // 4 - 1))
    mixed = jax.random.permutation(jax.random.fold_in(own, 3), amount)
    giver, receiver = mixed[0:amount // 2 * 2:2], mixed[1:amount // 2 * 2:2]
    room = jnp.minimum(sizes[giver] - 1, bound - sizes[receiver]) // 2
    room = jnp.where((giver == order[0]) | (receiver == order[0]) | (sizes[receiver] == 0), 0, jnp.maximum(room, 0))
    passed = jax.random.randint(jax.random.fold_in(own, 4), (amount // 2,), 0, 1 << 20) % (room + 1)
    sizes = sizes.at[giver].add(-passed).at[receiver].add(passed)
    items = jnp.searchsorted(jnp.cumsum(sizes), jnp.arange(rows * top), side="right").astype(jnp.int32)
    table = items.reshape(top, rows).T
    table = table[jax.random.permutation(jax.random.fold_in(own, 1), rows)]
    rotation = jax.random.randint(jax.random.fold_in(own, 2), (rows, 1), 0, top)
    return jnp.take_along_axis(table, (jnp.arange(top)[None, :] + rotation) % top, axis=1)


def shares(amount, total, bound, lean, full):
    weights = [(1 << 20) // math.isqrt(standing ** lean) + 1 for standing in range(1, amount + 1)]
    largest = bound if full else min(bound, max(-(-total // amount), total * weights[0] // sum(weights)))
    least = 1 if total - largest >= amount - 1 else 0
    counts, surplus = [largest] + [least] * (amount - 1), total - largest - least * (amount - 1)
    while surplus > 0:
        candidates = [i for i in range(1, amount) if counts[i] < largest] or [i for i in range(1, amount) if counts[i] < bound]
        mass, budget = sum([weights[i] for i in candidates]), surplus
        for i in candidates:
            addition = min(bound - counts[i], max(1, budget * weights[i] // mass), surplus)
            counts[i] = counts[i] + addition
            surplus = surplus - addition
    return np.array(counts)


def normal_values(rng, extent, deviation, bound, pieces=(), kind=jnp.bfloat16):
    level = levels(rng, extent, pieces, -0.22, 0.18) if pieces else 1.0
    array = jax.random.normal(rng, extent, jnp.float32) * deviation * level
    return jnp.minimum(jnp.maximum(array, -bound), bound).astype(kind)


def heavy_noise(key, extent, spread, reach, pieces, heavy, kind=jnp.bfloat16):
    result = spread * jax.random.normal(key, extent, jnp.float32)
    if pieces:
        result = result * levels(key, extent, pieces, -0.22, 0.18)
    return jnp.clip(spiked(result, jax.random.fold_in(key, 3), *heavy), -reach, reach).astype(kind)


def setup_inputs(seed: int = 0) -> dict:
    streams_of = jax.random.split(jax.random.key(seed), 6)
    route_ids_keys = jax.random.split(jax.random.fold_in(streams_of[0], 1), TOKENS // TOK_DEV)
    route_ids_turns = jax.random.permutation(jax.random.fold_in(streams_of[0], 3), TOKENS // TOK_DEV)
    route_ids = jax.vmap(lambda own, number: shared_out(jax.random.fold_in(streams_of[0], 2), own, number, TOK_DEV, EXPERTS, TOP, CAP, 2))(route_ids_keys, route_ids_turns).reshape((TOKENS, TOP))
    route_weights = jnp.clip(jnp.exp(math.log(0.5) - 3.218876 * jax.random.uniform(streams_of[1], (TOKENS, TOP), jnp.float32) ** levels(streams_of[1], (TOKENS, TOP), ((0, 768),), -0.2, 0.2)), 0.02, 0.5)
    hidden = heavy_noise(streams_of[2], (N_EDP, WIN, N_EP, CAP, FF), 1.0, 6.0, ((0, 48), (1, 16)), (0, 4, 48, 3.25))
    down_weight = normal_values(streams_of[3], (WIN, FF, D), FF ** -0.5, 0.3125, ((0, 16), (1, 48)))
    cotangent = normal_values(streams_of[4], (TOKENS, D), 1.0, 6.0, ((0, 768),))
    return dict(route_ids=route_ids, route_weights=route_weights, hidden=hidden, down_weight=down_weight, cotangent=cotangent)


def reference(route_ids, route_weights, hidden, down_weight, cotangent):
    experts_here = N_EP
    capacity = CAP
    groups = N_EDP
    ids_grouped = route_ids.reshape(groups, N_EP, TOK_DEV, TOP)
    probs_grouped = route_weights.reshape(groups, N_EP, TOK_DEV, TOP)
    cot_grouped = cotangent.reshape(groups, N_EP, TOK_DEV, D)
    weight_f32 = down_weight.astype(jnp.float32)
    labels = jnp.arange(experts_here, dtype=jnp.int32)
    source = jnp.arange(N_EP, dtype=jnp.int32)[:, None, None]

    def one_group(summed, inputs):
        ids_group, prob_group, cot_group, hid_group = inputs
        onehot = jnp.sum((ids_group[..., None] == labels).astype(jnp.int32), axis=2).astype(jnp.int32)
        preceding = (jnp.cumsum(onehot, axis=1) - onehot).astype(jnp.int32)
        flight = ids_group < experts_here
        expert = jnp.where(flight, ids_group, 0).astype(jnp.int32)
        slot_rank = jnp.take_along_axis(preceding, expert, axis=2).astype(jnp.int32)
        slot_index = ((expert * N_EP + source) * capacity + slot_rank).astype(jnp.int32)
        hid_f = hid_group.astype(jnp.float32)
        expert_out = jnp.einsum("escf,efd->escd", hid_f, weight_f32, precision=lax.Precision.HIGHEST).astype(jnp.bfloat16)
        lookup = expert_out.reshape(-1, D)
        picked = jnp.take(lookup, slot_index, axis=0).astype(jnp.float32)
        mixing = jnp.where(flight, prob_group, jnp.float32(0.0))
        combined = jnp.sum(mixing[..., None] * picked, axis=2).astype(jnp.bfloat16)
        cot_f = cot_group.astype(jnp.float32)
        route_grad = jnp.where(flight, jnp.sum(cot_f[:, :, None, :] * picked, axis=3), jnp.float32(0.0))
        weighted = mixing[..., None] * cot_f[:, :, None, :]
        slot_grad = jnp.zeros((experts_here * N_EP * capacity, D), jnp.float32)
        slot_grad = slot_grad.at[slot_index.reshape(-1)].add(weighted.reshape(-1, D))
        slot_grad = slot_grad.astype(jnp.bfloat16).reshape(experts_here, N_EP, capacity, D)
        grad_f = slot_grad.astype(jnp.float32)
        hidden_grad = jnp.einsum("escd,efd->escf", grad_f, weight_f32, precision=lax.Precision.HIGHEST).astype(jnp.bfloat16)
        summed = summed + jnp.einsum("escf,escd->efd", hid_f, grad_f, precision=lax.Precision.HIGHEST)
        return summed, (combined, route_grad, hidden_grad)

    start = jnp.zeros((experts_here, FF, D), jnp.float32)
    weight_grad, stacked = lax.scan(one_group, start, (ids_grouped, probs_grouped, cot_grouped, hidden))
    combined, route_grad, hidden_grad = stacked
    return (combined.reshape(TOKENS, D), route_grad.reshape(TOKENS, TOP), hidden_grad, weight_grad)
```

```python
import functools

import jax
import jax.numpy as jnp
from jax import lax
from jax.experimental import pallas as pl
from jax.experimental.pallas import tpu as pltpu
from jax.sharding import Mesh
from jax.sharding import PartitionSpec as P

AXES = ("z", "xl", "c", "y", "xh")
EDP = ("z", "xl", "c")
EP = ("y", "xh")
MESH = pl.DeviceIdType.MESH
F32 = jnp.float32
BF16 = jnp.bfloat16


def centred(i, n):
    half = n // 2
    return lax.rem(half + (2 * lax.rem(i, 2) - 1) * ((i + 1) // 2), n)


def kernel(
    sizes,
    ids_ref, w_ref, hid_ref, wsh_ref, cot_ref,
    lo_ref, rg_ref, hg_ref, wg_ref,
    sg, gin, eo, arr, hidb, wsw, wf, hgp, hgr, hgo, pf, xs, xr, zs, zr, fs, fr, matched, mixing,
    hid_s, hid_r, hid_l, wsw_s, wsw_r, wz_s, wz_r, wx_s, wx_r,
    g_s, g_r, g_l, o_s, o_r, o_l, hg_s, hg_r, rx_s, rx_r, rz_s, rz_r, f_s, f_r,
):
    nz, ny, nxh = sizes
    ne = ny * nxh
    cap, half = sg.shape[2], sg.shape[3]
    slots = ne * cap
    tokens, top = ids_ref.shape
    z, xl, c = lax.axis_index("z"), lax.axis_index("xl"), lax.axis_index("c")
    y, xh = lax.axis_index("y"), lax.axis_index("xh")
    me = y * nxh + xh
    core = 1 - c
    chip = z * 2 + xl

    def remote(src, dst, send, recv, **where):
        return pltpu.make_async_remote_copy(
            src_ref=src, dst_ref=dst, send_sem=send, recv_sem=recv,
            device_id=where, device_id_type=MESH,
        )

    barrier = pltpu.get_barrier_semaphore()

    def tell(**where):
        pl.semaphore_signal(barrier, inc=1, device_id=where, device_id_type=MESH)

    def tell_z(i, carry):
        tell(z=lax.rem(z + centred(i, nz), nz))
        return carry

    def tell_y(i, carry):
        yy = lax.rem(y + centred(i, ny), ny)
        for x in range(nxh):
            for h in range(2):
                tell(y=yy, xh=x, c=h)
        return carry

    lax.fori_loop(0, ny - 1, tell_y, 0)
    lax.fori_loop(0, nz - 1, tell_z, 0)
    tell(xl=1 - xl)
    for dx in range(1, nxh):
        for h in range(2):
            tell(xh=lax.rem(xh + dx, nxh), c=h)
    tell(c=core)
    peers = (ny - 1) * nxh * 2 + (nz - 1) + 1 + (nxh - 1) * 2 + 1

    ids = ids_ref[...]
    weights = w_ref[...]
    position = lax.broadcasted_iota(jnp.int32, (tokens, slots), 1)
    expert_of = position // cap
    rank_of = position - expert_of * cap
    names = jnp.zeros((tokens, slots), F32)
    chosen = jnp.zeros((tokens, slots), F32)
    for k in range(top):
        hit = ids[:, k : k + 1] == expert_of
        names = jnp.where(hit, 1.0, names)
        chosen = jnp.where(hit, weights[:, k : k + 1], chosen)
    row = lax.broadcasted_iota(jnp.int32, (tokens, tokens), 0)
    col = lax.broadcasted_iota(jnp.int32, (tokens, tokens), 1)
    before = jnp.where(col < row, 1.0, 0.0).astype(BF16)
    preceding = jnp.dot(before, names.astype(BF16), preferred_element_type=F32)
    match = jnp.where((names > 0.5) & (preceding == rank_of.astype(F32)), 1.0, 0.0)
    mix = match * chosen
    matched[...] = match
    mixing[...] = mix
    selector = match.T.astype(BF16)
    slot_weight = jnp.sum(mix.T, axis=1, keepdims=True)
    piece = min(half, 512)
    for h in range(2):
        for p in range(half // piece):
            at = h * half + p * piece
            picked = jnp.dot(selector, cot_ref[:, at : at + piece], preferred_element_type=F32)
            sg[h, :, :, p * piece : (p + 1) * piece] = (
                (picked * slot_weight).astype(BF16).reshape(ne, cap, piece)
            )

    pl.semaphore_wait(barrier, peers)

    other_half = pl.ds(pl.multiple_of(core * half, half), half)
    own_half = pl.ds(pl.multiple_of(c * half, half), half)
    swap = remote(wsh_ref.at[:, other_half], wsw, wsw_s, wsw_r, c=core)
    swap.start()
    share = remote(hid_ref, hidb.at[c], hid_s, hid_r, c=core)
    share.start()
    keep = pltpu.make_async_copy(hid_ref, hidb.at[c], hid_l)
    keep.start()

    def exchange(src, dst, send, recv, by_dest_core):
        slot = c * ne + me

        def to(yy, x, h):
            remote(src.at[h, yy * nxh + x], dst.at[slot], send, recv, y=yy, xh=x, c=h).start()

        def ring(i, carry):
            yy = lax.rem(y + centred(i, ny), ny)
            for x in range(nxh):
                for h in range(2):
                    to(yy, x, h)
            return carry

        lax.fori_loop(0, ny - 1, ring, 0)
        for dx in range(1, nxh):
            for h in range(2):
                to(y, lax.rem(xh + dx, nxh), h)
        to(y, xh, core)

    rest = 2 * ne - 1

    def all_of(ref, sem, count):
        pltpu.make_async_copy(ref.at[pl.ds(0, count)], ref.at[pl.ds(0, count)], sem).wait()

    swap.wait_recv()
    mine = wsh_ref[:, own_half].astype(F32)
    theirs = wsw[...].astype(F32)
    first = jnp.where(c == 0, mine, theirs)
    second = jnp.where(c == 0, theirs, mine)
    wf[chip] = jnp.concatenate([first, second], axis=0).astype(BF16)

    def spread(i, carry):
        d = centred(i, nz)
        remote(wf.at[chip], wf.at[chip], wz_s, wz_r.at[i], z=lax.rem(z + d, nz)).start()
        return carry

    lax.fori_loop(0, nz - 1, spread, 0)
    remote(wf.at[chip], wf.at[chip], wx_s, wx_r, xl=1 - xl).start()
    exchange(sg, gin, g_s, g_r, True)
    stay = pltpu.make_async_copy(sg.at[c, me], gin.at[c * ne + me], g_l)
    stay.start()

    def forward(i, carry):
        d = centred(i, nz)
        at = lax.rem(z - d + nz, nz) * 2 + xl
        remote(wf.at[at], wf.at[at], wz_s, wz_r.at[i], z=lax.rem(z + d, nz)).wait_recv()
        remote(wf.at[at], wf.at[at], wx_s, wx_r, xl=1 - xl).start()
        return carry

    lax.fori_loop(0, nz - 1, forward, 0)
    all_of(wf, wx_r, nz)
    share.wait_recv()
    keep.wait()

    ff = wf.shape[0] * wf.shape[1]

    def outputs(i, carry):
        n = pl.ds(pl.multiple_of(i * 256, 256), 256) if half >= 256 else slice(None)
        wide = min(half, 256)
        for h in range(2):
            got = jnp.dot(
                hidb[h], wf[:, :, n].reshape(ff, wide), preferred_element_type=F32
            )
            eo[h, :, :, n] = got.astype(BF16).reshape(ne, cap, wide)
        return carry

    lax.fori_loop(0, max(1, half // 256), outputs, 0)
    exchange(eo, arr, o_s, o_r, False)
    stay_out = pltpu.make_async_copy(eo.at[c, me], arr.at[c * ne + me], o_l)
    stay_out.start()

    all_of(gin, g_r, rest)
    stay.wait()

    def products(i, carry):
        n = pl.ds(pl.multiple_of(i * 256, 256), 256) if half >= 256 else slice(None)
        wide = min(half, 256)
        got = lax.dot_general(
            hidb[...].reshape(2 * slots, ff),
            gin[:, :, n].reshape(2 * slots, wide),
            (((0,), (0,)), ((), ())),
            preferred_element_type=F32,
        )
        pf[:, :, :, n] = got.reshape(*pf.shape[:3], wide)
        return carry

    lax.fori_loop(0, max(1, half // 256), products, 0)

    def to_neighbour(i, carry):
        to = lax.rem(z + centred(i, nz), nz)
        xs[to] = pf[to, 1 - xl].astype(BF16)
        remote(xs.at[to], xr.at[to], rx_s, rx_r.at[i], xl=1 - xl).start()
        return carry

    lax.fori_loop(0, nz, to_neighbour, 0)

    def hidden_term(group):
        rows = gin[pl.ds(group * ne, ne)].reshape(slots, half)
        return lax.dot_general(
            rows, wf[...].reshape(ff, half), (((1,), (1,)), ((), ())), preferred_element_type=F32
        )

    hgp[...] = hidden_term(core)
    give = remote(hgp, hgr, hg_s, hg_r, c=core)
    give.start()
    hgo[...] = hidden_term(c)

    def along_z(i, carry):
        to = lax.rem(z + centred(i, nz), nz)
        remote(xs.at[to], xr.at[to], rx_s, rx_r.at[i], xl=1 - xl).wait_recv()
        zs[to] = (pf[to, xl] + xr[to].astype(F32)).astype(BF16)
        remote(zs.at[to], zr.at[z], rz_s, rz_r, z=to).start()
        return carry

    lax.fori_loop(0, nz - 1, along_z, 0)
    remote(xs.at[z], xr.at[z], rx_s, rx_r.at[nz - 1], xl=1 - xl).wait_recv()
    total = pf[z, xl] + xr[z].astype(F32)

    give.wait_recv()
    hg_ref[...] = (hgo[...] + hgr[...]).astype(BF16)

    all_of(zr, rz_r, nz - 1)
    for d in range(1, nz):
        total = total + zr[lax.rem(z + d, nz)].astype(F32)
    rows = total.shape[0] // 2
    fs[...] = jnp.where(c == 0, total[rows:], total[:rows])
    finish = remote(fs, fr, f_s, f_r, c=core)
    finish.start()
    own_rows = jnp.where(c == 0, total[:rows], total[rows:])
    wg_ref[:, own_half] = own_rows
    finish.wait_recv()
    wg_ref[:, other_half] = fr[...]

    all_of(arr, o_r, rest)
    stay_out.wait()
    mix = mixing[...]
    high = mix.astype(BF16)
    low = (mix - high.astype(F32)).astype(BF16)
    table = jnp.concatenate([high, low], axis=0)
    for h in range(2):
        for p in range(half // piece):
            part = arr[h * ne : (h + 1) * ne, :, p * piece : (p + 1) * piece]
            both = jnp.dot(table, part.reshape(slots, piece), preferred_element_type=F32)
            at = h * half + p * piece
            lo_ref[:, at : at + piece] = (both[:tokens] + both[tokens:]).astype(BF16)
    scores = jnp.zeros((tokens, slots), F32)
    for h in range(2):
        scores = scores + lax.dot_general(
            cot_ref[:, h * half : (h + 1) * half],
            arr[h * ne : (h + 1) * ne].reshape(slots, half),
            (((1,), (1,)), ((), ())),
            preferred_element_type=F32,
        )
    scores = jnp.where(matched[...] > 0.5, scores, 0.0)
    lane = lax.broadcasted_iota(jnp.int32, (tokens, top), 1)
    grad = jnp.zeros((tokens, top), F32)
    for k in range(top):
        value = jnp.sum(
            jnp.where(ids[:, k : k + 1] == expert_of, scores, 0.0), axis=1, keepdims=True
        )
        grad = jnp.where(lane == k, value, grad)
    rg_ref[...] = grad

    swap.wait_send()
    share.wait_send()
    give.wait_send()
    finish.wait_send()
    all_of(wf, wz_s, nz - 1)
    all_of(wf, wx_s, nz)
    all_of(gin, g_s, rest)
    all_of(arr, o_s, rest)
    all_of(xs, rx_s, nz)
    all_of(zs, rz_s, nz - 1)


def solution(mesh):
    nz = mesh.shape["edp"] // 4
    ny = mesh.shape["ep"] // 2
    split = Mesh(mesh.devices.reshape(nz, 2, 2, ny, 2), AXES)

    def local(route_ids, route_weights, hidden, down_weight, cotangent):
        tokens, top = route_ids.shape
        ne, cap, ff = hidden.shape[2:]
        rows, features = down_weight.shape[1:]
        half = features // 2
        slots = ne * cap
        vmem = pl.BlockSpec(memory_space=pltpu.VMEM)
        dma = pltpu.SemaphoreType.DMA
        outs = pl.pallas_call(
            functools.partial(kernel, (nz, ny, 2)),
            out_shape=(
                jax.ShapeDtypeStruct((tokens, features), BF16),
                jax.ShapeDtypeStruct((tokens, top), F32),
                jax.ShapeDtypeStruct((slots, ff), BF16),
                jax.ShapeDtypeStruct((rows, features), F32),
            ),
            in_specs=[vmem] * 5,
            out_specs=(vmem,) * 4,
            scratch_shapes=[
                pltpu.VMEM((2, ne, cap, half), BF16),
                pltpu.VMEM((2 * ne, cap, half), BF16),
                pltpu.VMEM((2, ne, cap, half), BF16),
                pltpu.VMEM((2 * ne, cap, half), BF16),
                pltpu.VMEM((2, slots, ff), BF16),
                pltpu.VMEM((rows, half), BF16),
                pltpu.VMEM((2 * nz, 2 * rows, half), BF16),
                pltpu.VMEM((slots, ff), F32),
                pltpu.VMEM((slots, ff), F32),
                pltpu.VMEM((slots, ff), F32),
                pltpu.VMEM((nz, 2, 2 * rows, half), F32),
                pltpu.VMEM((nz, 2 * rows, half), BF16),
                pltpu.VMEM((nz, 2 * rows, half), BF16),
                pltpu.VMEM((nz, 2 * rows, half), BF16),
                pltpu.VMEM((nz, 2 * rows, half), BF16),
                pltpu.VMEM((rows, half), F32),
                pltpu.VMEM((rows, half), F32),
                pltpu.VMEM((tokens, slots), F32),
                pltpu.VMEM((tokens, slots), F32),
                dma, dma, dma,
                dma, dma,
                dma, dma((nz - 1,)), dma, dma,
                dma, dma, dma,
                dma, dma, dma,
                dma, dma,
                dma, dma((nz,)),
                dma, dma,
                dma, dma,
            ],
            compiler_params=pltpu.CompilerParams(
                collective_id=0, has_side_effects=True, vmem_limit_bytes=60 * 2**20
            ),
        )(
            route_ids,
            route_weights,
            hidden.reshape(slots, ff),
            down_weight.reshape(rows, features),
            cotangent,
        )
        out, route_grad, hidden_grad, weight_grad = outs
        return out, route_grad, hidden_grad.reshape(hidden.shape), weight_grad[None]

    placed = (P(AXES, None), P(AXES, None), P(EDP, EP, None, None, None), P(EP, EDP, None), P(AXES, None))
    return jax.shard_map(
        local,
        mesh=split,
        in_specs=placed,
        out_specs=(P(AXES, None), P(AXES, None), P(EDP, EP, None, None, None), P(EP, EDP, None)),
        check_vma=False,
    )
```

```python
import functools

import jax
import jax.numpy as jnp
from jax import lax
from jax.experimental import pallas as pl
from jax.experimental.pallas import tpu as pltpu
from jax.sharding import Mesh
from jax.sharding import PartitionSpec as P

AXES = ("z", "xl", "c", "y", "xh")
EDP = ("z", "xl", "c")
EP = ("y", "xh")
MESH = pl.DeviceIdType.MESH
F32 = jnp.float32
BF16 = jnp.bfloat16


ORDER = (1, -1, 4, -4, 2, -2, 3, -3, 5, -5, 6)


def centred(i, n):
    half = n // 2
    return lax.rem(half + (2 * lax.rem(i, 2) - 1) * ((i + 1) // 2), n)


def kernel(
    sizes,
    ids_ref, w_ref, hid_ref, wsh_ref, cot_ref,
    lo_ref, rg_ref, hg_ref, wg_ref,
    cot, own_w, sg, gin, eo, arr, hidb, wsw, wf, hgp, hgr, hgo, pf, xs, xr, zs, zr, fs, fr,
    matched, mixing,
    clear,
    cot_l, ow_l, hid_s, hid_r, hid_l, wsw_s, wsw_r, wz_s, wz_r, wx_s, wx_r,
    g_s, g_r, g_l, o_s, o_r, o_l, hg_s, hg_r, rx_s, rx_r, rz_s, rz_r, f_s, f_r,
):
    nz, ny, nxh, early = sizes
    chunks, _, ne, cap, wide = sg.shape
    half = chunks * wide
    slots = ne * cap
    top, tokens = ids_ref.shape
    ff = wf.shape[0] * wf.shape[1]
    z, xl, c = lax.axis_index("z"), lax.axis_index("xl"), lax.axis_index("c")
    y, xh = lax.axis_index("y"), lax.axis_index("xh")
    me = y * nxh + xh
    core = 1 - c
    chip = z * 2 + xl
    own_slot = c * ne + me

    def remote(src, dst, send, recv, **where):
        return pltpu.make_async_remote_copy(
            src_ref=src, dst_ref=dst, send_sem=send, recv_sem=recv,
            device_id=where, device_id_type=MESH,
        )

    def tell(sem, **where):
        pl.semaphore_signal(sem, inc=1, device_id=where, device_id_type=MESH)

    def all_of(ref, sem, count):
        pltpu.make_async_copy(ref.at[pl.ds(0, count)], ref.at[pl.ds(0, count)], sem).wait()

    barrier = pltpu.get_barrier_semaphore()

    def tell_y(i, carry):
        yy = lax.rem(y + centred(i, ny), ny)
        for x in range(nxh):
            for h in range(2):
                tell(barrier, y=yy, xh=x, c=h)
        return carry

    lax.fori_loop(0, ny - 1, tell_y, 0)
    for dx in range(1, nxh):
        for h in range(2):
            tell(barrier, xh=lax.rem(xh + dx, nxh), c=h)
    tell(barrier, xl=1 - xl)
    tell(barrier, c=core)

    late = z >= early

    def tell_z(i, carry):
        zz = lax.rem(z + centred(i, nz), nz)

        @pl.when((zz >= early) | jnp.logical_not(late))
        def _():
            tell(barrier, z=zz)

        return carry

    lax.fori_loop(0, nz - 1, tell_z, 0)
    plane = (ny - 1) * nxh * 2 + (nxh - 1) * 2 + 2
    peers = plane + jnp.where(late, nz - 1, early - 1)

    load_cot = pltpu.make_async_copy(cot_ref, cot, cot_l)
    load_cot.start()
    load_w = pltpu.make_async_copy(wsh_ref, own_w, ow_l)
    load_w.start()
    keep = pltpu.make_async_copy(hid_ref, hidb.at[c], hid_l)
    keep.start()

    ids = ids_ref[...]
    weights = w_ref[...]
    position = lax.broadcasted_iota(jnp.int32, (slots, tokens), 0)
    expert_of = position // cap
    rank_of = position - expert_of * cap
    names = jnp.zeros((slots, tokens), F32)
    chosen = jnp.zeros((slots, tokens), F32)
    for k in range(top):
        hit = ids[k : k + 1, :] == expert_of
        names = jnp.where(hit, 1.0, names)
        chosen = jnp.where(hit, weights[k : k + 1, :], chosen)
    row = lax.broadcasted_iota(jnp.int32, (tokens, tokens), 0)
    col = lax.broadcasted_iota(jnp.int32, (tokens, tokens), 1)
    before = jnp.where(row < col, 1.0, 0.0).astype(BF16)
    preceding = jnp.dot(names.astype(BF16), before, preferred_element_type=F32)
    match = jnp.where((names > 0.5) & (preceding == rank_of.astype(F32)), 1.0, 0.0)
    mix = match * chosen
    matched[...] = match
    selector = match.astype(BF16)
    slot_weight = jnp.sum(mix, axis=1, keepdims=True)
    load_cot.wait()

    def weigh(q):
        for h in range(2):
            at = h * half + q * wide
            picked = jnp.dot(selector, cot[:, at : at + wide], preferred_element_type=F32)
            sg[q, h] = (picked * slot_weight).astype(BF16).reshape(ne, cap, wide)

    weigh(0)

    pl.semaphore_wait(barrier, peers)

    @pl.when(late)
    def _():
        for zz in range(early):
            tell(clear, z=zz)

    load_w.wait()
    other_half = pl.ds(pl.multiple_of(core * half, half), half)
    own_half = pl.ds(pl.multiple_of(c * half, half), half)
    swap = remote(own_w.at[:, other_half], wsw, wsw_s, wsw_r, c=core)
    swap.start()

    def near(src, dst, send, recv):
        def ring(i, carry):
            yy = lax.rem(y + centred(i, ny), ny)
            for h in range(2):
                remote(src.at[h, yy * nxh + xh], dst.at[own_slot], send, recv, y=yy, c=h).start()
            return carry

        lax.fori_loop(0, ny - 1, ring, 0)
        remote(src.at[core, me], dst.at[own_slot], send, recv, c=core).start()

    def far_step(i, src, dst, send, recv):
        yy = lax.rem(y + centred(i, ny), ny)
        for dx in range(1, nxh):
            xx = lax.rem(xh + dx, nxh)
            for h in range(2):
                remote(
                    src.at[h, yy * nxh + xx], dst.at[own_slot], send, recv, y=yy, xh=xx, c=h
                ).start()

    def far(src, dst, send, recv):
        def ring(i, carry):
            far_step(i, src, dst, send, recv)
            return carry

        lax.fori_loop(0, ny, ring, 0)

    rest = 2 * ne - 1
    stay = [pltpu.make_async_copy(sg.at[q, c, me], gin.at[q, own_slot], g_l.at[q]) for q in range(chunks)]
    near(sg.at[0], gin.at[0], g_s, g_r.at[0])
    stay[0].start()
    far(sg.at[0], gin.at[0], g_s, g_r.at[0])
    share = remote(hid_ref, hidb.at[c], hid_s, hid_r, c=core)
    share.start()
    for q in range(1, chunks):
        weigh(q)
        near(sg.at[q], gin.at[q], g_s, g_r.at[q])
        stay[q].start()
        far(sg.at[q], gin.at[q], g_s, g_r.at[q])

    swap.wait_recv()
    mine = own_w[:, own_half].astype(F32)
    theirs = wsw[...].astype(F32)
    first = jnp.where(c == 0, mine, theirs)
    second = jnp.where(c == 0, theirs, mine)
    wf[chip] = jnp.concatenate([first, second], axis=0).astype(BF16)
    remote(wf.at[chip], wf.at[chip], wx_s, wx_r, xl=1 - xl).start()
    mixing[...] = mix.T

    @pl.when(jnp.logical_not(late))
    def _():
        pl.semaphore_wait(clear, nz - early)

    def pass_on(piece, d, step):
        remote(
            wf.at[piece], wf.at[piece], wz_s, wz_r.at[ORDER.index(d)], z=lax.rem(z + step + nz, nz)
        ).start()

    for d in (4, -4, 1, -1):
        pass_on(chip, d, d)
    last = chunks - 1

    for i, d in enumerate(ORDER):
        at = lax.rem(z - d + nz, nz) * 2 + xl
        remote(wf.at[at], wf.at[at], wz_s, wz_r.at[i], xl=1 - xl).wait_recv()
        if abs(d) == 1:
            pass_on(at, 2 * d, d)
        if abs(d) == 4:
            sign = d // 4
            pass_on(at, 5 * sign, sign)
            pass_on(at, 3 * sign, -sign)

            @pl.when(c == (1 - sign) // 2)
            def _():
                pass_on(at, 6, 2 * sign)

        remote(wf.at[at], wf.at[at], wx_s, wx_r, xl=1 - xl).start()

    def products(q):
        step = min(wide, 256)

        def body(i, carry):
            n = pl.ds(pl.multiple_of(i * step, step), step)
            got = lax.dot_general(
                hidb[...].reshape(2 * slots, ff),
                gin[q, :, :, n].reshape(2 * slots, step),
                (((0,), (0,)), ((), ())),
                preferred_element_type=F32,
            )
            pf[q, :, :, :, n] = got.reshape(nz, 2, pf.shape[3], step)
            return carry

        lax.fori_loop(0, wide // step, body, 0)

        def to_neighbour(i, carry):
            to = lax.rem(z + centred(i, nz), nz)
            xs[q, to] = pf[q, to, 1 - xl].astype(BF16)
            remote(xs.at[q, to], xr.at[q, to], rx_s, rx_r.at[q, i], xl=1 - xl).start()
            return carry

        lax.fori_loop(0, nz, to_neighbour, 0)

    def along_z(q):
        def body(i, carry):
            to = lax.rem(z + centred(i, nz), nz)
            remote(xs.at[q, to], xr.at[q, to], rx_s, rx_r.at[q, i], xl=1 - xl).wait_recv()
            zs[q, to] = (pf[q, to, xl] + xr[q, to].astype(F32)).astype(BF16)
            remote(zs.at[q, to], zr.at[q, z], rz_s, rz_r.at[q], z=to).start()
            return carry

        lax.fori_loop(0, nz - 1, body, 0)

    def outputs():
        step = min(half, 256)

        def body(i, carry):
            n = pl.ds(pl.multiple_of(i * step, step), step)
            for h in range(2):
                got = jnp.dot(
                    hidb[h], wf[:, :, n].reshape(ff, step), preferred_element_type=F32
                )
                eo[h, :, :, n] = got.astype(BF16).reshape(ne, cap, step)
            return carry

        lax.fori_loop(0, half // step, body, 0)

    share.wait_recv()
    keep.wait()
    for q in range(chunks):
        all_of(gin.at[q], g_r.at[q], rest)
        stay[q].wait()
        if q == last:
            near(eo, arr, o_s, o_r)
        products(q)
        if q == 0:
            all_of(wf, wx_r, nz)
            outputs()
        if q < chunks - 1:
            along_z(q)
    stay_out = pltpu.make_async_copy(eo.at[c, me], arr.at[own_slot], o_l)
    stay_out.start()
    far(eo, arr, o_s, o_r)
    along_z(last)

    def hidden_term(group):
        got = jnp.zeros((slots, ff), F32)
        for q in range(chunks):
            rows = gin[q, pl.ds(group * ne, ne)].reshape(slots, wide)
            cols = wf[:, :, q * wide : (q + 1) * wide].reshape(ff, wide)
            got = got + lax.dot_general(
                rows, cols, (((1,), (1,)), ((), ())), preferred_element_type=F32
            )
        return got

    hgp[...] = hidden_term(core)
    give = remote(hgp, hgr, hg_s, hg_r, c=core)
    give.start()
    hgo[...] = hidden_term(c)
    give.wait_recv()
    hg_ref[...] = (hgo[...] + hgr[...]).astype(BF16)

    rows = fs.shape[0]
    for q in range(chunks):
        remote(
            xs.at[q, z], xr.at[q, z], rx_s, rx_r.at[q, nz - 1], xl=1 - xl
        ).wait_recv()
        total = pf[q, z, xl] + xr[q, z].astype(F32)
        all_of(zr.at[q], rz_r.at[q], nz - 1)
        for d in range(1, nz):
            total = total + zr[q, lax.rem(z + d, nz)].astype(F32)
        fs[:, q * wide : (q + 1) * wide] = jnp.where(c == 0, total[rows:], total[:rows])
        at = pl.multiple_of(c * half + q * wide, wide)
        wg_ref[:, pl.ds(at, wide)] = jnp.where(c == 0, total[:rows], total[rows:])
    finish = remote(fs, fr, f_s, f_r, c=core)
    finish.start()

    all_of(arr, o_r, rest)
    stay_out.wait()
    mix = mixing[...]
    high = mix.astype(BF16)
    low = (mix - high.astype(F32)).astype(BF16)
    table = jnp.concatenate([high, low], axis=0)
    piece = min(half, 512)
    for h in range(2):
        for p in range(half // piece):
            part = arr[h * ne : (h + 1) * ne, :, p * piece : (p + 1) * piece]
            both = jnp.dot(table, part.reshape(slots, piece), preferred_element_type=F32)
            at = h * half + p * piece
            lo_ref[:, at : at + piece] = (both[:tokens] + both[tokens:]).astype(BF16)
    scores = jnp.zeros((slots, tokens), F32)
    for h in range(2):
        scores = scores + lax.dot_general(
            arr[h * ne : (h + 1) * ne].reshape(slots, half),
            cot[:, h * half : (h + 1) * half],
            (((1,), (1,)), ((), ())),
            preferred_element_type=F32,
        )
    scores = jnp.where(matched[...] > 0.5, scores, 0.0)
    for k in range(top):
        rg_ref[k : k + 1, :] = jnp.sum(
            jnp.where(ids_ref[k : k + 1, :] == expert_of, scores, 0.0), axis=0, keepdims=True
        )
    finish.wait_recv()
    wg_ref[:, other_half] = fr[...]

    swap.wait_send()
    share.wait_send()
    give.wait_send()
    finish.wait_send()
    all_of(wf, wz_s, nz - 1)
    all_of(wf, wx_s, nz)
    for q in range(chunks):
        all_of(gin.at[q], g_s, rest)
        all_of(xs.at[q], rx_s, nz)
        all_of(zs.at[q], rz_s, nz - 1)
    all_of(arr, o_s, rest)


def solution(mesh):
    nz = mesh.shape["edp"] // 4
    ny = mesh.shape["ep"] // 2
    chunks = 2
    split = Mesh(mesh.devices.reshape(nz, 2, 2, ny, 2), AXES)

    def local(route_ids, route_weights, hidden, down_weight, cotangent):
        tokens, top = route_ids.shape
        ne, cap, ff = hidden.shape[2:]
        rows, features = down_weight.shape[1:]
        half = features // 2
        wide = half // chunks
        slots = ne * cap
        vmem = pl.BlockSpec(memory_space=pltpu.VMEM)
        away = pl.BlockSpec(memory_space=pltpu.HBM)
        dma = pltpu.SemaphoreType.DMA
        terms = (chunks, nz, 2 * rows, wide)
        outs = pl.pallas_call(
            functools.partial(kernel, (nz, ny, 2, min(5, nz // 2))),
            out_shape=(
                jax.ShapeDtypeStruct((tokens, features), BF16),
                jax.ShapeDtypeStruct((top, tokens), F32),
                jax.ShapeDtypeStruct((slots, ff), BF16),
                jax.ShapeDtypeStruct((rows, features), F32),
            ),
            in_specs=[vmem, vmem, away, away, away],
            out_specs=(vmem,) * 4,
            scratch_shapes=[
                pltpu.VMEM((tokens, features), BF16),
                pltpu.VMEM((rows, features), BF16),
                pltpu.VMEM((chunks, 2, ne, cap, wide), BF16),
                pltpu.VMEM((chunks, 2 * ne, cap, wide), BF16),
                pltpu.VMEM((2, ne, cap, half), BF16),
                pltpu.VMEM((2 * ne, cap, half), BF16),
                pltpu.VMEM((2, slots, ff), BF16),
                pltpu.VMEM((rows, half), BF16),
                pltpu.VMEM((2 * nz, 2 * rows, half), BF16),
                pltpu.VMEM((slots, ff), F32),
                pltpu.VMEM((slots, ff), F32),
                pltpu.VMEM((slots, ff), F32),
                pltpu.VMEM((chunks, nz, 2, 2 * rows, wide), F32),
                pltpu.VMEM(terms, BF16),
                pltpu.VMEM(terms, BF16),
                pltpu.VMEM(terms, BF16),
                pltpu.VMEM(terms, BF16),
                pltpu.VMEM((rows, half), F32),
                pltpu.VMEM((rows, half), F32),
                pltpu.VMEM((slots, tokens), F32),
                pltpu.VMEM((tokens, slots), F32),
                pltpu.SemaphoreType.REGULAR,
                dma, dma,
                dma, dma, dma,
                dma, dma,
                dma, dma((nz - 1,)), dma, dma,
                dma, dma((chunks,)), dma((chunks,)),
                dma, dma, dma,
                dma, dma,
                dma, dma((chunks, nz)),
                dma, dma((chunks,)),
                dma, dma,
            ],
            compiler_params=pltpu.CompilerParams(
                collective_id=0, has_side_effects=True, vmem_limit_bytes=40 * 2**20
            ),
        )(
            pltpu.with_memory_space_constraint(route_ids.T, pltpu.HBM),
            pltpu.with_memory_space_constraint(route_weights.T, pltpu.HBM),
            pltpu.with_memory_space_constraint(hidden.reshape(slots, ff), pltpu.HBM),
            pltpu.with_memory_space_constraint(down_weight.reshape(rows, features), pltpu.HBM),
            pltpu.with_memory_space_constraint(cotangent, pltpu.HBM),
        )
        out, route_grad, hidden_grad, weight_grad = outs
        return out, route_grad.T, hidden_grad.reshape(hidden.shape), weight_grad[None]

    placed = (P(AXES, None), P(AXES, None), P(EDP, EP, None, None, None), P(EP, EDP, None), P(AXES, None))
    return jax.shard_map(
        local,
        mesh=split,
        in_specs=placed,
        out_specs=(P(AXES, None), P(AXES, None), P(EDP, EP, None, None, None), P(EP, EDP, None)),
        check_vma=False,
    )
```

```python
import functools

import jax
import jax.numpy as jnp
from jax import lax
from jax.experimental import pallas as pl
from jax.experimental.pallas import tpu as pltpu
from jax.sharding import Mesh
from jax.sharding import PartitionSpec as P

AXES = ("z", "xl", "c", "y", "xh")
EDP = ("z", "xl", "c")
EP = ("y", "xh")
MESH = pl.DeviceIdType.MESH
F32 = jnp.float32
BF16 = jnp.bfloat16


ORDER = (1, -1, 4, -4, 2, -2, 3, -3, 5, -5, 6)


FAR_FIRST = True
OUT_FIRST = True
CHUNKS = 1


def centred(i, n):
    half = n // 2
    return lax.rem(half + (2 * lax.rem(i, 2) - 1) * ((i + 1) // 2), n)


def kernel(
    sizes,
    ids_ref, w_ref, hid_ref, wsh_ref, cot_ref,
    lo_ref, rg_ref, hg_ref, wg_ref,
    cot, own_w, sg, gin, eo, arr, hidb, wsw, wf, hgp, hgr, hgo, pf, xs, xr, zs, zr, fs, fr,
    matched, mixing,
    clear,
    cot_l, ow_l, hid_s, hid_r, hid_l, wsw_s, wsw_r, wz_s, wz_r, wx_s, wx_r,
    g_s, g_r, g_l, o_s, o_r, o_l, hg_s, hg_r, rx_s, rx_r, rz_s, rz_r, f_s, f_r,
):
    nz, ny, nxh, early = sizes
    chunks, _, ne, cap, wide = sg.shape
    half = chunks * wide
    slots = ne * cap
    top, tokens = ids_ref.shape
    ff = wf.shape[0] * wf.shape[1]
    z, xl, c = lax.axis_index("z"), lax.axis_index("xl"), lax.axis_index("c")
    y, xh = lax.axis_index("y"), lax.axis_index("xh")
    me = y * nxh + xh
    core = 1 - c
    chip = z * 2 + xl
    own_slot = c * ne + me

    def remote(src, dst, send, recv, **where):
        return pltpu.make_async_remote_copy(
            src_ref=src, dst_ref=dst, send_sem=send, recv_sem=recv,
            device_id=where, device_id_type=MESH,
        )

    def tell(sem, **where):
        pl.semaphore_signal(sem, inc=1, device_id=where, device_id_type=MESH)

    def all_of(ref, sem, count):
        pltpu.make_async_copy(ref.at[pl.ds(0, count)], ref.at[pl.ds(0, count)], sem).wait()

    barrier = pltpu.get_barrier_semaphore()

    def tell_y(i, carry):
        yy = lax.rem(y + centred(i, ny), ny)
        for x in range(nxh):
            for h in range(2):
                tell(barrier, y=yy, xh=x, c=h)
        return carry

    lax.fori_loop(0, ny - 1, tell_y, 0)
    for dx in range(1, nxh):
        for h in range(2):
            tell(barrier, xh=lax.rem(xh + dx, nxh), c=h)
    tell(barrier, xl=1 - xl)
    tell(barrier, c=core)

    late = z >= early

    def tell_z(i, carry):
        zz = lax.rem(z + centred(i, nz), nz)

        @pl.when((zz >= early) | (zz > z))
        def _():
            tell(barrier, z=zz)

        return carry

    lax.fori_loop(0, nz - 1, tell_z, 0)
    plane = (ny - 1) * nxh * 2 + (nxh - 1) * 2 + 2
    peers = plane + jnp.where(late, nz - 1, z)

    load_cot = pltpu.make_async_copy(cot_ref, cot, cot_l)
    load_cot.start()
    load_w = pltpu.make_async_copy(wsh_ref, own_w, ow_l)
    load_w.start()
    keep = pltpu.make_async_copy(hid_ref, hidb.at[c], hid_l)
    keep.start()

    ids = ids_ref[...]
    weights = w_ref[...]
    position = lax.broadcasted_iota(jnp.int32, (slots, tokens), 0)
    expert_of = position // cap
    rank_of = position - expert_of * cap
    names = jnp.zeros((slots, tokens), F32)
    chosen = jnp.zeros((slots, tokens), F32)
    for k in range(top):
        hit = ids[k : k + 1, :] == expert_of
        names = jnp.where(hit, 1.0, names)
        chosen = jnp.where(hit, weights[k : k + 1, :], chosen)
    row = lax.broadcasted_iota(jnp.int32, (tokens, tokens), 0)
    col = lax.broadcasted_iota(jnp.int32, (tokens, tokens), 1)
    before = jnp.where(row < col, 1.0, 0.0).astype(BF16)
    preceding = jnp.dot(names.astype(BF16), before, preferred_element_type=F32)
    match = jnp.where((names > 0.5) & (preceding == rank_of.astype(F32)), 1.0, 0.0)
    mix = match * chosen
    matched[...] = match
    selector = match.astype(BF16)
    slot_weight = jnp.sum(mix, axis=1, keepdims=True)
    load_cot.wait()

    def weigh(q):
        for h in range(2):
            at = h * half + q * wide
            picked = jnp.dot(selector, cot[:, at : at + wide], preferred_element_type=F32)
            sg[q, h] = (picked * slot_weight).astype(BF16).reshape(ne, cap, wide)

    weigh(0)

    pl.semaphore_wait(barrier, peers)

    for zz in range(early):

        @pl.when(z > zz)
        def _():
            tell(clear, z=zz)

    load_w.wait()
    other_half = pl.ds(pl.multiple_of(core * half, half), half)
    own_half = pl.ds(pl.multiple_of(c * half, half), half)
    swap = remote(own_w.at[:, other_half], wsw, wsw_s, wsw_r, c=core)
    swap.start()

    def near(src, dst, send, recv):
        def ring(i, carry):
            yy = lax.rem(y + centred(i, ny), ny)
            for h in range(2):
                remote(src.at[h, yy * nxh + xh], dst.at[own_slot], send, recv, y=yy, c=h).start()
            return carry

        lax.fori_loop(0, ny - 1, ring, 0)
        remote(src.at[core, me], dst.at[own_slot], send, recv, c=core).start()

    def far_step(i, src, dst, send, recv):
        yy = lax.rem(y + centred(i, ny), ny)
        for dx in range(1, nxh):
            xx = lax.rem(xh + dx, nxh)
            for h in range(2):
                remote(
                    src.at[h, yy * nxh + xx], dst.at[own_slot], send, recv, y=yy, xh=xx, c=h
                ).start()

    def far(src, dst, send, recv):
        def ring(i, carry):
            far_step(i, src, dst, send, recv)
            return carry

        lax.fori_loop(0, ny, ring, 0)

    rest = 2 * ne - 1
    stay = [pltpu.make_async_copy(sg.at[q, c, me], gin.at[q, own_slot], g_l.at[q]) for q in range(chunks)]

    def send_chunk(q):
        if FAR_FIRST:
            far(sg.at[q], gin.at[q], g_s, g_r.at[q])
        near(sg.at[q], gin.at[q], g_s, g_r.at[q])
        stay[q].start()
        if not FAR_FIRST:
            far(sg.at[q], gin.at[q], g_s, g_r.at[q])

    send_chunk(0)
    swap.wait_recv()
    mine = own_w[:, own_half].astype(F32)
    theirs = wsw[...].astype(F32)
    first = jnp.where(c == 0, mine, theirs)
    second = jnp.where(c == 0, theirs, mine)
    wf[chip] = jnp.concatenate([first, second], axis=0).astype(BF16)
    remote(wf.at[chip], wf.at[chip], wx_s, wx_r, xl=1 - xl).start()

    def pass_on(piece, d, step):
        remote(
            wf.at[piece], wf.at[piece], wz_s, wz_r.at[ORDER.index(d)], z=lax.rem(z + step + nz, nz)
        ).start()

    @pl.when(late)
    def _():
        for d in (4, -4, 1, -1):
            pass_on(chip, d, d)

    share = remote(hid_ref, hidb.at[c], hid_s, hid_r, c=core)
    share.start()
    for q in range(1, chunks):
        weigh(q)
        send_chunk(q)
    mixing[...] = mix.T

    @pl.when(jnp.logical_not(late))
    def _():
        pl.semaphore_wait(clear, nz - 1 - z)
        for d in (4, -4, 1, -1):
            pass_on(chip, d, d)

    last = chunks - 1

    for i, d in enumerate(ORDER):
        at = lax.rem(z - d + nz, nz) * 2 + xl
        remote(wf.at[at], wf.at[at], wz_s, wz_r.at[i], xl=1 - xl).wait_recv()
        if abs(d) == 1:
            pass_on(at, 2 * d, d)
        if abs(d) == 4:
            sign = d // 4
            pass_on(at, 5 * sign, sign)
            pass_on(at, 3 * sign, -sign)

            @pl.when(c == (1 - sign) // 2)
            def _():
                pass_on(at, 6, 2 * sign)

        remote(wf.at[at], wf.at[at], wx_s, wx_r, xl=1 - xl).start()

    def products(q):
        step = min(wide, 256)

        def body(i, carry):
            n = pl.ds(pl.multiple_of(i * step, step), step)
            got = lax.dot_general(
                hidb[...].reshape(2 * slots, ff),
                gin[q, :, :, n].reshape(2 * slots, step),
                (((0,), (0,)), ((), ())),
                preferred_element_type=F32,
            )
            pf[q, :, :, :, n] = got.reshape(nz, 2, pf.shape[3], step)
            return carry

        lax.fori_loop(0, wide // step, body, 0)

        def to_neighbour(i, carry):
            to = lax.rem(z + centred(i, nz), nz)
            xs[q, to] = pf[q, to, 1 - xl].astype(BF16)
            remote(xs.at[q, to], xr.at[q, to], rx_s, rx_r.at[q, i], xl=1 - xl).start()
            return carry

        lax.fori_loop(0, nz, to_neighbour, 0)

    def along_z(q):
        def body(i, carry):
            to = lax.rem(z + centred(i, nz), nz)
            remote(xs.at[q, to], xr.at[q, to], rx_s, rx_r.at[q, i], xl=1 - xl).wait_recv()
            zs[q, to] = (pf[q, to, xl] + xr[q, to].astype(F32)).astype(BF16)
            remote(zs.at[q, to], zr.at[q, z], rz_s, rz_r.at[q], z=to).start()
            return carry

        lax.fori_loop(0, nz - 1, body, 0)

    def outputs():
        step = min(half, 256)

        def body(i, carry):
            n = pl.ds(pl.multiple_of(i * step, step), step)
            for h in range(2):
                got = jnp.dot(
                    hidb[h], wf[:, :, n].reshape(ff, step), preferred_element_type=F32
                )
                eo[h, :, :, n] = got.astype(BF16).reshape(ne, cap, step)
            return carry

        lax.fori_loop(0, half // step, body, 0)

    share.wait_recv()
    keep.wait()
    stay_out = pltpu.make_async_copy(eo.at[c, me], arr.at[own_slot], o_l)
    if OUT_FIRST:
        all_of(wf, wx_r, nz)
        outputs()
        near(eo, arr, o_s, o_r)
        stay_out.start()
    for q in range(chunks):
        all_of(gin.at[q], g_r.at[q], rest)
        stay[q].wait()
        if q == last and not OUT_FIRST:
            near(eo, arr, o_s, o_r)
            stay_out.start()
        products(q)
        if q == 0 and not OUT_FIRST:
            all_of(wf, wx_r, nz)
            outputs()
        if q < last:
            along_z(q)
    far(eo, arr, o_s, o_r)
    along_z(last)

    def hidden_term(group):
        got = jnp.zeros((slots, ff), F32)
        for q in range(chunks):
            rows = gin[q, pl.ds(group * ne, ne)].reshape(slots, wide)
            cols = wf[:, :, q * wide : (q + 1) * wide].reshape(ff, wide)
            got = got + lax.dot_general(
                rows, cols, (((1,), (1,)), ((), ())), preferred_element_type=F32
            )
        return got

    hgp[...] = hidden_term(core)
    give = remote(hgp, hgr, hg_s, hg_r, c=core)
    give.start()
    hgo[...] = hidden_term(c)
    give.wait_recv()
    hg_ref[...] = (hgo[...] + hgr[...]).astype(BF16)

    rows = fs.shape[0]
    for q in range(chunks):
        remote(
            xs.at[q, z], xr.at[q, z], rx_s, rx_r.at[q, nz - 1], xl=1 - xl
        ).wait_recv()
        total = pf[q, z, xl] + xr[q, z].astype(F32)
        all_of(zr.at[q], rz_r.at[q], nz - 1)
        for d in range(1, nz):
            total = total + zr[q, lax.rem(z + d, nz)].astype(F32)
        fs[:, q * wide : (q + 1) * wide] = jnp.where(c == 0, total[rows:], total[:rows])
        at = pl.multiple_of(c * half + q * wide, wide)
        wg_ref[:, pl.ds(at, wide)] = jnp.where(c == 0, total[:rows], total[rows:])
    finish = remote(fs, fr, f_s, f_r, c=core)
    finish.start()

    all_of(arr, o_r, rest)
    stay_out.wait()
    mix = mixing[...]
    high = mix.astype(BF16)
    low = (mix - high.astype(F32)).astype(BF16)
    table = jnp.concatenate([high, low], axis=0)
    piece = min(half, 512)
    for h in range(2):
        for p in range(half // piece):
            part = arr[h * ne : (h + 1) * ne, :, p * piece : (p + 1) * piece]
            both = jnp.dot(table, part.reshape(slots, piece), preferred_element_type=F32)
            at = h * half + p * piece
            lo_ref[:, at : at + piece] = (both[:tokens] + both[tokens:]).astype(BF16)
    scores = jnp.zeros((slots, tokens), F32)
    for h in range(2):
        scores = scores + lax.dot_general(
            arr[h * ne : (h + 1) * ne].reshape(slots, half),
            cot[:, h * half : (h + 1) * half],
            (((1,), (1,)), ((), ())),
            preferred_element_type=F32,
        )
    scores = jnp.where(matched[...] > 0.5, scores, 0.0)
    for k in range(top):
        rg_ref[k : k + 1, :] = jnp.sum(
            jnp.where(ids_ref[k : k + 1, :] == expert_of, scores, 0.0), axis=0, keepdims=True
        )
    finish.wait_recv()
    wg_ref[:, other_half] = fr[...]

    swap.wait_send()
    share.wait_send()
    give.wait_send()
    finish.wait_send()
    all_of(wf, wz_s, nz - 1)
    all_of(wf, wx_s, nz)
    for q in range(chunks):
        all_of(gin.at[q], g_s, rest)
        all_of(xs.at[q], rx_s, nz)
        all_of(zs.at[q], rz_s, nz - 1)
    all_of(arr, o_s, rest)


def put(*refs):
    for i in range(4):
        refs[4 + i][...] = refs[i][...]


def solution(mesh):
    nz = mesh.shape["edp"] // 4
    ny = mesh.shape["ep"] // 2
    chunks = CHUNKS
    split = Mesh(mesh.devices.reshape(nz, 2, 2, ny, 2), AXES)

    def local(route_ids, route_weights, hidden, down_weight, cotangent):
        tokens, top = route_ids.shape
        ne, cap, ff = hidden.shape[2:]
        rows, features = down_weight.shape[1:]
        half = features // 2
        wide = half // chunks
        slots = ne * cap
        vmem = pl.BlockSpec(memory_space=pltpu.VMEM)
        away = pl.BlockSpec(memory_space=pl.ANY)
        dma = pltpu.SemaphoreType.DMA
        terms = (chunks, nz, 2 * rows, wide)
        outs = pl.pallas_call(
            functools.partial(kernel, (nz, ny, 2, min(5, nz // 2))),
            out_shape=(
                jax.ShapeDtypeStruct((tokens, features), BF16),
                jax.ShapeDtypeStruct((top, tokens), F32),
                jax.ShapeDtypeStruct((slots, ff), BF16),
                jax.ShapeDtypeStruct((rows, features), F32),
            ),
            in_specs=[vmem, vmem, away, away, away],
            out_specs=(vmem,) * 4,
            scratch_shapes=[
                pltpu.VMEM((tokens, features), BF16),
                pltpu.VMEM((rows, features), BF16),
                pltpu.VMEM((chunks, 2, ne, cap, wide), BF16),
                pltpu.VMEM((chunks, 2 * ne, cap, wide), BF16),
                pltpu.VMEM((2, ne, cap, half), BF16),
                pltpu.VMEM((2 * ne, cap, half), BF16),
                pltpu.VMEM((2, slots, ff), BF16),
                pltpu.VMEM((rows, half), BF16),
                pltpu.VMEM((2 * nz, 2 * rows, half), BF16),
                pltpu.VMEM((slots, ff), F32),
                pltpu.VMEM((slots, ff), F32),
                pltpu.VMEM((slots, ff), F32),
                pltpu.VMEM((chunks, nz, 2, 2 * rows, wide), F32),
                pltpu.VMEM(terms, BF16),
                pltpu.VMEM(terms, BF16),
                pltpu.VMEM(terms, BF16),
                pltpu.VMEM(terms, BF16),
                pltpu.VMEM((rows, half), F32),
                pltpu.VMEM((rows, half), F32),
                pltpu.VMEM((slots, tokens), F32),
                pltpu.VMEM((tokens, slots), F32),
                pltpu.SemaphoreType.REGULAR,
                dma, dma,
                dma, dma, dma,
                dma, dma,
                dma, dma((nz - 1,)), dma, dma,
                dma, dma((chunks,)), dma((chunks,)),
                dma, dma, dma,
                dma, dma,
                dma, dma((chunks, nz)),
                dma, dma((chunks,)),
                dma, dma,
            ],
            compiler_params=pltpu.CompilerParams(
                collective_id=0, has_side_effects=True, vmem_limit_bytes=40 * 2**20
            ),
        )(
            pltpu.with_memory_space_constraint(route_ids.T, pltpu.HBM),
            pltpu.with_memory_space_constraint(route_weights.T, pltpu.HBM),
            pltpu.with_memory_space_constraint(hidden.reshape(slots, ff), pltpu.HBM),
            pltpu.with_memory_space_constraint(down_weight.reshape(rows, features), pltpu.HBM),
            pltpu.with_memory_space_constraint(cotangent, pltpu.HBM),
        )
        out, route_grad, hidden_grad, weight_grad = pl.pallas_call(
            put,
            out_shape=tuple(jax.ShapeDtypeStruct(o.shape, o.dtype) for o in outs),
            in_specs=[vmem] * 4,
            out_specs=(vmem,) * 4,
            compiler_params=pltpu.CompilerParams(vmem_limit_bytes=8 * 2**20),
            name="put",
        )(*outs)
        return out, route_grad.T, hidden_grad.reshape(hidden.shape), weight_grad[None]

    placed = (P(AXES, None), P(AXES, None), P(EDP, EP, None, None, None), P(EP, EDP, None), P(AXES, None))
    return jax.shard_map(
        local,
        mesh=split,
        in_specs=placed,
        out_specs=(P(AXES, None), P(AXES, None), P(EDP, EP, None, None, None), P(EP, EDP, None)),
        check_vma=False,
    )
```

```python
import functools

import jax
import jax.numpy as jnp
from jax import lax
from jax.experimental import pallas as pl
from jax.experimental.pallas import tpu as pltpu
from jax.sharding import Mesh
from jax.sharding import PartitionSpec as P

AXES = ("z", "xl", "c", "y", "xh")
EDP = ("z", "xl", "c")
EP = ("y", "xh")
MESH = pl.DeviceIdType.MESH
F32 = jnp.float32
BF16 = jnp.bfloat16


ORDER = (1, -1, 4, -4, 3, -3, 5, -5, 6, 2, -2)
SIDE = (1, -1, 2, -2)
CROSS = (4, -4, 3, -3, 5, -5, 6)


OUT_FIRST = True
CHUNKS = 1


def centred(i, n):
    half = n // 2
    return lax.rem(half + (2 * lax.rem(i, 2) - 1) * ((i + 1) // 2), n)


def kernel(
    sizes,
    ids_ref, w_ref, hid_ref, wsh_ref, cot_ref,
    lo_ref, rg_ref, hg_ref, wg_ref,
    cot, own_w, sg, gin, eo, arr, hidb, wsw, wf, hgp, hgr, hgo, pf, xs, xr, zs, zr, fs, fr,
    matched, mixing, sums,
    clear, hello,
    cot_l, ow_l, hid_s, hid_r, hid_l, wsw_s, wsw_r, wz_s, wz_r, wx_s, wx_r, wx_o, wy_r,
    g_s, g_r, g_l, o_s, o_r, o_l, hg_s, hg_r, rx_s, rx_r, rz_s, rz_r, f_s, f_r,
):
    nz, ny, nxh, early = sizes
    chunks, _, ne, cap, wide = sg.shape
    half = chunks * wide
    slots = ne * cap
    top, tokens = ids_ref.shape
    ff = wf.shape[0] * wf.shape[1]
    z, xl, c = lax.axis_index("z"), lax.axis_index("xl"), lax.axis_index("c")
    y, xh = lax.axis_index("y"), lax.axis_index("xh")
    me = y * nxh + xh
    core = 1 - c
    chip = z * 2 + xl
    own_slot = c * ne + me

    def remote(src, dst, send, recv, **where):
        return pltpu.make_async_remote_copy(
            src_ref=src, dst_ref=dst, send_sem=send, recv_sem=recv,
            device_id=where, device_id_type=MESH,
        )

    def tell(sem, **where):
        pl.semaphore_signal(sem, inc=1, device_id=where, device_id_type=MESH)

    def all_of(ref, sem, count):
        pltpu.make_async_copy(ref.at[pl.ds(0, count)], ref.at[pl.ds(0, count)], sem).wait()

    barrier = pltpu.get_barrier_semaphore()
    corner = (z == 0) & (xl == 0)
    column = (xl == 0) & (c == 0) & (y == 0) & (xh == 0)
    is_first = corner & column
    group = corner & jnp.logical_not(is_first)
    beside = (z == 0) & (xl == 1) & (c == 0) & (y == 0) & (xh == 0)
    late = (z >= early) | is_first

    @pl.when(jnp.logical_not(is_first))
    def _():
        def tell_y(i, carry):
            yy = lax.rem(y + centred(i, ny), ny)
            for x in range(nxh):
                for h in range(2):
                    tell(barrier, y=yy, xh=x, c=h)
            return carry

        lax.fori_loop(0, ny - 1, tell_y, 0)
        for dx in range(1, nxh):
            for h in range(2):
                tell(barrier, xh=lax.rem(xh + dx, nxh), c=h)
        tell(barrier, xl=1 - xl)
        tell(barrier, c=core)

    def tell_z(i, carry):
        zz = lax.rem(z + centred(i, nz), nz)

        @pl.when((zz >= early) | ((zz > z) & jnp.logical_not(is_first)) | (column & (zz == 0)))
        def _():
            tell(barrier, z=zz)

        return carry

    lax.fori_loop(0, nz - 1, tell_z, 0)
    plane = (ny - 1) * nxh * 2 + (nxh - 1) * 2 + 2 - jnp.where(group | beside, 1, 0)
    ahead = z - jnp.where(column, 1, 0)
    peers = plane + jnp.where(late, nz - 1, ahead)

    load_cot = pltpu.make_async_copy(cot_ref, cot, cot_l)
    load_cot.start()
    load_w = pltpu.make_async_copy(wsh_ref, own_w, ow_l)
    load_w.start()
    keep = pltpu.make_async_copy(hid_ref, hidb.at[c], hid_l)
    keep.start()

    ids = ids_ref[...]
    weights = w_ref[...]
    position = lax.broadcasted_iota(jnp.int32, (slots, tokens), 0)
    expert_of = position // cap
    rank_of = position - expert_of * cap
    names = jnp.zeros((slots, tokens), F32)
    chosen = jnp.zeros((slots, tokens), F32)
    for k in range(top):
        hit = ids[k : k + 1, :] == expert_of
        names = jnp.where(hit, 1.0, names)
        chosen = jnp.where(hit, weights[k : k + 1, :], chosen)
    row = lax.broadcasted_iota(jnp.int32, (tokens, tokens), 0)
    col = lax.broadcasted_iota(jnp.int32, (tokens, tokens), 1)
    before = jnp.where(row < col, 1.0, 0.0).astype(BF16)
    preceding = jnp.dot(names.astype(BF16), before, preferred_element_type=F32)
    match = jnp.where((names > 0.5) & (preceding == rank_of.astype(F32)), 1.0, 0.0)
    mix = match * chosen
    matched[...] = match.reshape(ne, cap, tokens)
    selector = match.astype(BF16)
    slot_weight = jnp.sum(mix, axis=1, keepdims=True)
    load_cot.wait()

    def weigh(q):
        for h in range(2):
            at = h * half + q * wide
            picked = jnp.dot(selector, cot[:, at : at + wide], preferred_element_type=F32)
            sg[q, h] = (picked * slot_weight).astype(BF16).reshape(ne, cap, wide)

    weigh(0)

    pl.semaphore_wait(barrier, peers)

    for zz in range(early):
        here = (z > zz) | (is_first & (zz > 0))
        if zz == 0:
            here = here & jnp.logical_not(column)

        @pl.when(here)
        def _():
            tell(clear, z=zz)

    @pl.when(is_first)
    def _():
        for yy in range(ny):
            for x in range(nxh):
                for h in range(2):
                    if (yy, x, h) != (0, 0, 0):
                        tell(hello, y=yy, xh=x, c=h)
        tell(hello, xl=1 - xl)

    load_w.wait()
    other_half = pl.ds(pl.multiple_of(core * half, half), half)
    own_half = pl.ds(pl.multiple_of(c * half, half), half)
    swap = remote(own_w.at[:, other_half], wsw, wsw_s, wsw_r, c=core)

    @pl.when(jnp.logical_not(group))
    def _():
        swap.start()

    def near(src, dst, send, recv, skip=False):
        def to(yy, h, where):
            def go():
                remote(src.at[h, yy * nxh + xh], dst.at[own_slot], send, recv, **where).start()

            if skip:
                pl.when(jnp.logical_not(corner & (yy == 0) & (xh == 0) & (h == 0)))(go)
            else:
                go()

        def ring(i, carry):
            yy = lax.rem(y + centred(i, ny), ny)
            for h in range(2):
                to(yy, h, dict(y=yy, c=h))
            return carry

        lax.fori_loop(0, ny - 1, ring, 0)
        to(y, core, dict(c=core))

    def far(src, dst, send, recv, skip=False):
        def ring(i, carry):
            yy = lax.rem(y + centred(i, ny), ny)
            for dx in range(1, nxh):
                xx = lax.rem(xh + dx, nxh)
                for h in range(2):

                    def go():
                        remote(
                            src.at[h, yy * nxh + xx], dst.at[own_slot], send, recv, y=yy, xh=xx, c=h
                        ).start()

                    if skip and h == 0:
                        pl.when(jnp.logical_not(corner & (yy == 0) & (xx == 0)))(go)
                    else:
                        go()
            return carry

        lax.fori_loop(0, ny, ring, 0)

    rest = 2 * ne - 1
    stay = [pltpu.make_async_copy(sg.at[q, c, me], gin.at[q, own_slot], g_l.at[q]) for q in range(chunks)]

    def send_chunk(q, skip=False):
        far(sg.at[q], gin.at[q], g_s, g_r.at[q], skip)
        near(sg.at[q], gin.at[q], g_s, g_r.at[q], skip)
        stay[q].start()

    send_chunk(0, True)

    @pl.when(group | beside)
    def _():
        pl.semaphore_wait(hello, 1)

    @pl.when(group)
    def _():
        remote(
            sg.at[0, 0, 0], gin.at[0, own_slot], g_s, g_r.at[0],
            z=z, xl=xl, c=c * 0, y=y * 0, xh=xh * 0,
        ).start()
        swap.start()

    swap.wait_recv()
    mine = own_w[:, own_half].astype(F32)
    theirs = wsw[...].astype(F32)
    first = jnp.where(c == 0, mine, theirs)
    second = jnp.where(c == 0, theirs, mine)
    wf[chip] = jnp.concatenate([first, second], axis=0).astype(BF16)
    remote(wf.at[chip], wf.at[chip], wx_s, wx_o, xl=1 - xl).start()

    def pass_on(piece, d, step):
        remote(
            wf.at[piece], wf.at[piece], wz_s, wz_r.at[ORDER.index(d)], z=lax.rem(z + step + nz, nz)
        ).start()

    @pl.when(late)
    def _():
        for d in (4, -4, 1, -1):
            pass_on(chip, d, d)

    share = remote(hid_ref, hidb.at[c], hid_s, hid_r, c=core)
    share.start()
    for q in range(1, chunks):
        weigh(q)
        send_chunk(q)
    mixing[...] = mix.reshape(ne, cap, tokens)

    @pl.when(jnp.logical_not(late))
    def _():
        pl.semaphore_wait(clear, nz - 1 - ahead)
        for d in (4, -4, 1, -1):
            pass_on(chip, d, d)

    last = chunks - 1

    def side(piece, d, step):
        remote(
            wf.at[piece], wf.at[piece], wz_s, wy_r.at[SIDE.index(d)], z=lax.rem(z + step + nz, nz)
        ).start()

    def piece_from(d, column):
        return lax.rem(z - d + nz, nz) * 2 + column

    remote(wf.at[chip], wf.at[chip], wx_s, wx_o, xl=1 - xl).wait_recv()
    for d in (1, -1):
        side(z * 2 + 1 - xl, d, d)

    for i, d in enumerate(ORDER):
        at = piece_from(d, xl)
        remote(wf.at[at], wf.at[at], wz_s, wz_r.at[i], xl=1 - xl).wait_recv()
        if abs(d) == 1:
            pass_on(at, 2 * d, d)
        if abs(d) == 4:
            sign = d // 4
            pass_on(at, 5 * sign, sign)
            pass_on(at, 3 * sign, -sign)

            @pl.when(c == (1 - sign) // 2)
            def _():
                pass_on(at, 6, 2 * sign)

        if d in CROSS:
            remote(wf.at[at], wf.at[at], wx_s, wx_r, xl=1 - xl).start()
        if d == -4:
            for k, e in enumerate(SIDE[:2]):
                at = piece_from(e, 1 - xl)
                remote(wf.at[at], wf.at[at], wz_s, wy_r.at[k], xl=1 - xl).wait_recv()
                side(at, 2 * e, e)

    for k, e in enumerate(SIDE[2:]):
        at = piece_from(e, 1 - xl)
        remote(wf.at[at], wf.at[at], wz_s, wy_r.at[2 + k], xl=1 - xl).wait_recv()

    def taker(i):
        others = nz - early
        served = jnp.where(
            i < early, lax.rem(z + i, early), early + lax.rem(z + 1 + i - 2 * early + others, others)
        )
        return jnp.where(z >= early, served, lax.rem(z + centred(i, nz), nz))

    def products(q):
        step = min(wide, 256)

        def body(i, carry):
            n = pl.ds(pl.multiple_of(i * step, step), step)
            got = lax.dot_general(
                hidb[...].reshape(2 * slots, ff),
                gin[q, :, :, n].reshape(2 * slots, step),
                (((0,), (0,)), ((), ())),
                preferred_element_type=F32,
            )
            pf[q, :, :, :, n] = got.reshape(nz, 2, pf.shape[3], step)
            return carry

        lax.fori_loop(0, wide // step, body, 0)

        def to_neighbour(i, carry):
            to = taker(i)
            xs[q, to] = pf[q, to, 1 - xl].astype(BF16)
            remote(xs.at[q, to], xr.at[q, to], rx_s, rx_r.at[q, i], xl=1 - xl).start()
            return carry

        lax.fori_loop(0, nz, to_neighbour, 0)

    def along_z(q):
        def body(i, carry):
            to = taker(i)
            remote(xs.at[q, to], xr.at[q, to], rx_s, rx_r.at[q, i], xl=1 - xl).wait_recv()
            zs[q, to] = (pf[q, to, xl] + xr[q, to].astype(F32)).astype(BF16)
            remote(zs.at[q, to], zr.at[q, z], rz_s, rz_r.at[q], z=to).start()
            return carry

        lax.fori_loop(0, nz - 1, body, 0)

    def outputs():
        step = min(half, 256)

        def body(i, carry):
            n = pl.ds(pl.multiple_of(i * step, step), step)
            for h in range(2):
                got = jnp.dot(
                    hidb[h], wf[:, :, n].reshape(ff, step), preferred_element_type=F32
                )
                eo[h, :, :, n] = got.astype(BF16).reshape(ne, cap, step)
            return carry

        lax.fori_loop(0, half // step, body, 0)

    share.wait_recv()
    keep.wait()
    stay_out = pltpu.make_async_copy(eo.at[c, me], arr.at[own_slot], o_l)
    if OUT_FIRST:
        all_of(wf, wx_r, len(CROSS))
        outputs()
        near(eo, arr, o_s, o_r.at[0])
        far(eo, arr, o_s, o_r.at[1])
        stay_out.start()
    for q in range(chunks):
        all_of(gin.at[q], g_r.at[q], rest)
        stay[q].wait()
        if q == last and not OUT_FIRST:
            near(eo, arr, o_s, o_r.at[0])
            stay_out.start()
        products(q)
        if q == 0 and not OUT_FIRST:
            all_of(wf, wx_r, len(CROSS))
            outputs()
        if q < last:
            along_z(q)
    along_z(last)

    def hidden_term(group):
        got = jnp.zeros((slots, ff), F32)
        for q in range(chunks):
            rows = gin[q, pl.ds(group * ne, ne)].reshape(slots, wide)
            cols = wf[:, :, q * wide : (q + 1) * wide].reshape(ff, wide)
            got = got + lax.dot_general(
                rows, cols, (((1,), (1,)), ((), ())), preferred_element_type=F32
            )
        return got

    hgp[...] = hidden_term(core)
    give = remote(hgp, hgr, hg_s, hg_r, c=core)
    give.start()
    hgo[...] = hidden_term(c)
    give.wait_recv()
    hg_ref[...] = (hgo[...] + hgr[...]).astype(BF16)

    def combine(column, first):
        def rows_of(ref, base=0):
            return jnp.concatenate([ref[base + e * nxh + column] for e in range(ny)], axis=0)

        part_slots = ny * cap
        mixed = rows_of(mixing).T
        high = mixed.astype(BF16)
        low = (mixed - high.astype(F32)).astype(BF16)
        table = jnp.concatenate([high, low], axis=0)
        scores = jnp.zeros((part_slots, tokens), F32)
        for h in range(2):
            part = rows_of(arr, h * ne)
            cols = slice(h * half, (h + 1) * half)
            both = jnp.dot(table, part, preferred_element_type=F32)
            value = both[:tokens] + both[tokens:]
            if first:
                sums[:, cols] = value
            else:
                lo_ref[:, cols] = (sums[:, cols] + value).astype(BF16)
            scores = scores + lax.dot_general(
                part, cot[:, cols], (((1,), (1,)), ((), ())), preferred_element_type=F32
            )
        scores = jnp.where(rows_of(matched) > 0.5, scores, 0.0)
        name = lax.broadcasted_iota(jnp.int32, (part_slots, tokens), 0) // cap * nxh + column
        for k in range(top):
            value = jnp.sum(
                jnp.where(ids_ref[k : k + 1, :] == name, scores, 0.0), axis=0, keepdims=True
            )
            rg_ref[k : k + 1, :] = value if first else rg_ref[k : k + 1, :] + value

    all_of(arr, o_r.at[0], 2 * ny - 1)
    stay_out.wait()
    combine(xh, True)

    rows = fs.shape[0]
    for q in range(chunks):
        remote(
            xs.at[q, z], xr.at[q, z], rx_s, rx_r.at[q, nz - 1], xl=1 - xl
        ).wait_recv()
        total = pf[q, z, xl] + xr[q, z].astype(F32)
        all_of(zr.at[q], rz_r.at[q], nz - 1)
        for d in range(1, nz):
            total = total + zr[q, lax.rem(z + d, nz)].astype(F32)
        fs[:, q * wide : (q + 1) * wide] = jnp.where(c == 0, total[rows:], total[:rows])
        at = pl.multiple_of(c * half + q * wide, wide)
        wg_ref[:, pl.ds(at, wide)] = jnp.where(c == 0, total[:rows], total[rows:])
    finish = remote(fs, fr, f_s, f_r, c=core)
    finish.start()

    all_of(arr, o_r.at[1], 2 * ny)
    combine(1 - xh, False)
    finish.wait_recv()
    wg_ref[:, other_half] = fr[...]

    swap.wait_send()
    share.wait_send()
    give.wait_send()
    finish.wait_send()
    all_of(wf, wz_s, nz - 1 + len(SIDE))
    all_of(wf, wx_s, 1 + len(CROSS))
    for q in range(chunks):
        all_of(gin.at[q], g_s, rest)
        all_of(xs.at[q], rx_s, nz)
        all_of(zs.at[q], rz_s, nz - 1)
    all_of(arr, o_s, rest)


def put(*refs):
    for i in range(4):
        refs[4 + i][...] = refs[i][...]


def solution(mesh):
    nz = mesh.shape["edp"] // 4
    ny = mesh.shape["ep"] // 2
    chunks = CHUNKS
    split = Mesh(mesh.devices.reshape(nz, 2, 2, ny, 2), AXES)

    def local(route_ids, route_weights, hidden, down_weight, cotangent):
        tokens, top = route_ids.shape
        ne, cap, ff = hidden.shape[2:]
        rows, features = down_weight.shape[1:]
        half = features // 2
        wide = half // chunks
        slots = ne * cap
        vmem = pl.BlockSpec(memory_space=pltpu.VMEM)
        away = pl.BlockSpec(memory_space=pl.ANY)
        dma = pltpu.SemaphoreType.DMA
        terms = (chunks, nz, 2 * rows, wide)
        outs = pl.pallas_call(
            functools.partial(kernel, (nz, ny, 2, min(5, nz // 2))),
            out_shape=(
                jax.ShapeDtypeStruct((tokens, features), BF16),
                jax.ShapeDtypeStruct((top, tokens), F32),
                jax.ShapeDtypeStruct((slots, ff), BF16),
                jax.ShapeDtypeStruct((rows, features), F32),
            ),
            in_specs=[vmem, vmem, away, away, away],
            out_specs=(vmem,) * 4,
            scratch_shapes=[
                pltpu.VMEM((tokens, features), BF16),
                pltpu.VMEM((rows, features), BF16),
                pltpu.VMEM((chunks, 2, ne, cap, wide), BF16),
                pltpu.VMEM((chunks, 2 * ne, cap, wide), BF16),
                pltpu.VMEM((2, ne, cap, half), BF16),
                pltpu.VMEM((2 * ne, cap, half), BF16),
                pltpu.VMEM((2, slots, ff), BF16),
                pltpu.VMEM((rows, half), BF16),
                pltpu.VMEM((2 * nz, 2 * rows, half), BF16),
                pltpu.VMEM((slots, ff), F32),
                pltpu.VMEM((slots, ff), F32),
                pltpu.VMEM((slots, ff), F32),
                pltpu.VMEM((chunks, nz, 2, 2 * rows, wide), F32),
                pltpu.VMEM(terms, BF16),
                pltpu.VMEM(terms, BF16),
                pltpu.VMEM(terms, BF16),
                pltpu.VMEM(terms, BF16),
                pltpu.VMEM((rows, half), F32),
                pltpu.VMEM((rows, half), F32),
                pltpu.VMEM((ne, cap, tokens), F32),
                pltpu.VMEM((ne, cap, tokens), F32),
                pltpu.VMEM((tokens, features), F32),
                pltpu.SemaphoreType.REGULAR,
                pltpu.SemaphoreType.REGULAR,
                dma, dma,
                dma, dma, dma,
                dma, dma,
                dma, dma((nz - 1,)), dma, dma, dma, dma((4,)),
                dma, dma((chunks,)), dma((chunks,)),
                dma, dma((2,)), dma,
                dma, dma,
                dma, dma((chunks, nz)),
                dma, dma((chunks,)),
                dma, dma,
            ],
            compiler_params=pltpu.CompilerParams(
                collective_id=0, has_side_effects=True, vmem_limit_bytes=40 * 2**20
            ),
        )(
            pltpu.with_memory_space_constraint(route_ids.T, pltpu.HBM),
            pltpu.with_memory_space_constraint(route_weights.T, pltpu.HBM),
            pltpu.with_memory_space_constraint(hidden.reshape(slots, ff), pltpu.HBM),
            pltpu.with_memory_space_constraint(down_weight.reshape(rows, features), pltpu.HBM),
            pltpu.with_memory_space_constraint(cotangent, pltpu.HBM),
        )
        out, route_grad, hidden_grad, weight_grad = pl.pallas_call(
            put,
            out_shape=tuple(jax.ShapeDtypeStruct(o.shape, o.dtype) for o in outs),
            in_specs=[vmem] * 4,
            out_specs=(vmem,) * 4,
            compiler_params=pltpu.CompilerParams(vmem_limit_bytes=8 * 2**20),
            name="put",
        )(*outs)
        return out, route_grad.T, hidden_grad.reshape(hidden.shape), weight_grad[None]

    placed = (P(AXES, None), P(AXES, None), P(EDP, EP, None, None, None), P(EP, EDP, None), P(AXES, None))
    return jax.shard_map(
        local,
        mesh=split,
        in_specs=placed,
        out_specs=(P(AXES, None), P(AXES, None), P(EDP, EP, None, None, None), P(EP, EDP, None)),
        check_vma=False,
    )
```
